32 devices in a mesh: pipe: 1, expert: 32 (over z, y, x, core).
Axes of the slice: x: 2, y: 2, z: 4, core: 2. Of those that a mesh axis runs over, the one named last changes fastest.
Arguments:
- inputs: bfloat16 [1, 2, 2048, 2048], P('pipe', None, 'expert'), may hold values from -6 to 6
- grads_out: bfloat16 [1, 2, 2048, 2048], P('pipe', None, 'expert'), may hold values from -6 to 6
- expert_ids: int32 [1, 2, 2048, 6], P('pipe', None, 'expert'), may hold values from 0 to 31, all different within a row; in each aligned block of 64 rows (0 to 63, 64 to 127, ..., all dimensions but the last counted through in order) at most 32 rows name the same one
- gate_values: float32 [1, 2, 2048, 6], P('pipe', None, 'expert'), may hold values from 0.1 to 0.5
- w_gate: bfloat16 [1, 32, 2048, 768], P('pipe', 'expert'), may hold values from -0.125 to 0.125
- w_up: bfloat16 [1, 32, 2048, 768], P('pipe', 'expert'), may hold values from -0.125 to 0.125
- w_down: bfloat16 [1, 32, 768, 2048], P('pipe', 'expert'), may hold values from -0.21875 to 0.21875
Outputs:
- received: bfloat16 [1, 2, 2048, 2048], P('pipe', None, 'expert')
- gate_grad: float32 [1, 2, 2048, 6], P('pipe', None, 'expert')
The draws below stay inside these ranges and needn't reach their ends.
Inputs may be any that keep to these rules, and one draw needn't show every extreme that they name: `expert_ids`: each row names 6 different experts. Within the 64 rows of one device for one section and micro-batch, no expert is named by more than 32 rows, a bound that some expert reaches in some of these blocks.
All inputs are finite; a program needn't handle non-finite values.
Results may differ from the reference program's by a relative error of at most 0.0041.
Values may be sent and summed in bfloat16 or wider, within the bound.
A program may use at most 128 MiB of HBM per device.

```python
import math
import jax
import jax.numpy as jnp
import numpy as np
from jax import lax

D = 2048
H = 768
TOP = 6
MB = 2
TOK_DEV = 64
SECTIONS = 1
EXPERTS = 32
TOKENS = 2048
CAP = 32


def block_levels(stream_key, dims, shards, least, high):
    def one(axis_at, shards_of):
        steps = jax.random.uniform(jax.random.fold_in(jax.random.fold_in(stream_key, 6), axis_at), (shards_of,), jnp.float32, least / len(shards), high / len(shards))
        return jnp.repeat(jnp.exp(steps), dims[axis_at] // shards_of).reshape((-1,) + (1,) * (len(dims) - axis_at - 1))

    gain = one(*shards[0])
    for cut in shards[1:]:
        gain = gain * one(*cut)
    return gain


def deal_out(stream_key, own, number, rows, amount, top, bound, lean):
    ranking = jax.random.permutation(stream_key, amount)
    packed, usual = shares(amount, rows * top, bound, lean, True), shares(amount, rows * top, bound, lean, False)
    places = jnp.arange(amount)

    def named(lengths, offset_by):
        used = int((lengths > 0).sum())
        fixed = max(1, used // 4)
        passed = fixed + (places - fixed + offset_by * (used - fixed)) % max(1, amount - fixed)
        return jnp.zeros((amount,), jnp.int32).at[ranking[jnp.where(places < fixed, places, passed)]].set(jnp.asarray(lengths, jnp.int32))

    lengths = jnp.where(number % 4 == 0, named(packed, number // 4), named(usual, number - number // 4 - 1))
    mixed = jax.random.permutation(jax.random.fold_in(own, 3), amount)
    source_of, taker = mixed[0:amount // 2 * 2:2], mixed[1:amount // 2 * 2:2]
    room = jnp.minimum(lengths[source_of] - 1, bound - lengths[taker]) // 2
    room = jnp.where((source_of == ranking[0]) | (taker == ranking[0]) | (lengths[taker] == 0), 0, jnp.maximum(room, 0))
    passed = jax.random.randint(jax.random.fold_in(own, 4), (amount // 2,), 0, 1 << 20) % (room + 1)
    lengths = lengths.at[source_of].add(-passed).at[taker].add(passed)
    members = jnp.searchsorted(jnp.cumsum(lengths), jnp.arange(rows * top), side="right").astype(jnp.int32)
    listing = members.reshape(top, rows).T
    listing = listing[jax.random.permutation(jax.random.fold_in(own, 1), rows)]
    offset_by = jax.random.randint(jax.random.fold_in(own, 2), (rows, 1), 0, top)
    return jnp.take_along_axis(listing, (jnp.arange(top)[None, :] + offset_by) % top, axis=1)


def shares(number_of, total, reach, slope, full):
    loads = [(1 << 20) // math.isqrt(standing ** slope) + 1 for standing in range(1, number_of + 1)]
    largest = reach if full else min(reach, max(-(-total // number_of), total * loads[0] // sum(loads)))
    least = 1 if total - largest >= number_of - 1 else 0
    holding, spare = [largest] + [least] * (number_of - 1), total - largest - least * (number_of - 1)
    while spare > 0:
        candidates = [i for i in range(1, number_of) if holding[i] < largest] or [i for i in range(1, number_of) if holding[i] < reach]
        mass, budget = sum([loads[i] for i in candidates]), spare
        for i in candidates:
            more = min(reach - holding[i], max(1, budget * loads[i] // mass), spare)
            holding[i] = holding[i] + more
            spare = spare - more
    return np.array(holding)


def centred(stream_key, shape, deviation, bound, split=(), kind=jnp.bfloat16):
    level = block_levels(stream_key, shape, split, -0.22, 0.18) if split else 1.0
    result = jax.random.normal(stream_key, shape, jnp.float32) * deviation * level
    return jnp.minimum(jnp.maximum(result, -bound), bound).astype(kind)


def setup_inputs(seed: int = 0) -> dict:
    seeds = jax.random.split(jax.random.key(seed), 8)
    inputs = centred(seeds[0], (SECTIONS, MB, TOKENS, D), 1.0, 6.0, ((2, 32),))
    grads_out = centred(seeds[1], (SECTIONS, MB, TOKENS, D), 1.0, 6.0, ((2, 32),))
    expert_ids_keys = jax.random.split(jax.random.fold_in(seeds[2], 1), SECTIONS * MB * TOKENS // TOK_DEV)
    expert_ids_turns = jax.random.permutation(jax.random.fold_in(seeds[2], 3), SECTIONS * MB * TOKENS // TOK_DEV)
    expert_ids = jax.vmap(lambda own, number: deal_out(jax.random.fold_in(seeds[2], 2), own, number, TOK_DEV, EXPERTS, TOP, CAP, 2))(expert_ids_keys, expert_ids_turns).reshape((SECTIONS, MB, TOKENS, TOP))
    gate_values = jnp.clip(0.1 + 0.4 * jax.random.uniform(seeds[3], (SECTIONS, MB, TOKENS, TOP), jnp.float32) ** block_levels(seeds[3], (SECTIONS, MB, TOKENS, TOP), ((2, 32),), -0.2, 0.2), 0.1, 0.5)
    w_gate = centred(seeds[4], (SECTIONS, EXPERTS, D, H), D ** -0.5, 0.125, ((1, 32),))
    w_up = centred(seeds[5], (SECTIONS, EXPERTS, D, H), D ** -0.5, 0.125, ((1, 32),))
    w_down = centred(seeds[6], (SECTIONS, EXPERTS, H, D), H ** -0.5, 0.21875, ((1, 32),))
    return {"inputs": inputs, "grads_out": grads_out, "expert_ids": expert_ids, "gate_values": gate_values, "w_gate": w_gate, "w_up": w_up, "w_down": w_down}


def expert_rows(x_rows, grad_rows, gate_weight, up_weight, down_weight):
    gate_pre = jnp.dot(x_rows, gate_weight, preferred_element_type=jnp.float32)
    up_pre = jnp.dot(x_rows, up_weight, preferred_element_type=jnp.float32)
    back_grad = lax.dot_general(grad_rows, down_weight, (((1,), (1,)), ((), ())), preferred_element_type=jnp.float32)
    logistic = jax.nn.sigmoid(gate_pre)
    swish = gate_pre * logistic
    score = jnp.sum(back_grad * swish * up_pre, axis=1).astype(jnp.bfloat16)
    d_gate = (back_grad * up_pre * logistic * (1.0 + gate_pre * (1.0 - logistic))).astype(jnp.bfloat16)
    d_up = (back_grad * swish).astype(jnp.bfloat16)
    pair_grad = lax.dot_general(d_gate, gate_weight, (((1,), (1,)), ((), ())), preferred_element_type=jnp.float32)
    pair_grad = pair_grad + lax.dot_general(d_up, up_weight, (((1,), (1,)), ((), ())), preferred_element_type=jnp.float32)
    return pair_grad.astype(jnp.bfloat16), score


def section_pass(x_rows, grad_rows, ids, gates, gate_all, up_all, down_all):
    pair_count = TOKENS * TOP
    block_rows = 128
    flat_ids = ids.reshape(pair_count).astype(jnp.int32)
    onehot = (flat_ids[:, None] == jnp.arange(EXPERTS, dtype=jnp.int32)[None, :]).astype(jnp.int32)
    counts = jnp.sum(onehot, axis=0).astype(jnp.int32)
    group_span = ((counts + block_rows - 1) // block_rows * block_rows).astype(jnp.int32)
    starts = (jnp.cumsum(group_span) - group_span).astype(jnp.int32)
    group_end = (starts + group_span).astype(jnp.int32)
    position = jnp.sum((jnp.cumsum(onehot, axis=0) - onehot) * onehot, axis=1).astype(jnp.int32)
    target = (starts[flat_ids] + position).astype(jnp.int32)
    buffer_rows = (pair_count // block_rows + EXPERTS + 1) * block_rows
    token_of = jnp.arange(pair_count, dtype=jnp.int32) // TOP
    buffer_x = jnp.zeros((buffer_rows, D), jnp.bfloat16).at[target].set(x_rows[token_of])
    buffer_grad = jnp.zeros((buffer_rows, D), jnp.bfloat16).at[target].set(grad_rows[token_of])
    block_count = buffer_rows // block_rows
    block_start = jnp.arange(block_count, dtype=jnp.int32) * block_rows
    owner_expert = jnp.sum((group_end[None, :] <= block_start[:, None]).astype(jnp.int32), axis=1).astype(jnp.int32)
    owner_expert = jnp.minimum(owner_expert, EXPERTS - 1).astype(jnp.int32)

    def one_block(index):
        first_row = (index * block_rows).astype(jnp.int32)
        chosen = owner_expert[index]
        return expert_rows(lax.dynamic_slice_in_dim(buffer_x, first_row, block_rows, 0),
                           lax.dynamic_slice_in_dim(buffer_grad, first_row, block_rows, 0),
                           gate_all[chosen], up_all[chosen], down_all[chosen])

    block_grads, block_scores = lax.map(one_block, jnp.arange(block_count, dtype=jnp.int32))
    block_grads = block_grads.reshape(buffer_rows, D)
    block_scores = block_scores.reshape(buffer_rows)
    pair_grad = block_grads[target].reshape(TOKENS, TOP, D).astype(jnp.float32)
    pair_score = block_scores[target].reshape(TOKENS, TOP).astype(jnp.float32)
    input_grad = grad_rows.astype(jnp.float32) + jnp.sum(gates[:, :, None].astype(jnp.float32) * pair_grad, axis=1)
    return input_grad.astype(jnp.bfloat16), pair_score


def reference(inputs, grads_out, expert_ids, gate_values, w_gate, w_up, w_down):
    all_grads = []
    all_scores = []
    for section in range(SECTIONS):
        grad_list = []
        score_list = []
        for micro in range(MB):
            input_grad, pair_score = section_pass(inputs[section, micro], grads_out[section, micro],
                                                  expert_ids[section, micro], gate_values[section, micro],
                                                  w_gate[section], w_up[section], w_down[section])
            grad_list.append(input_grad)
            score_list.append(pair_score)
        all_grads.append(jnp.stack(grad_list))
        all_scores.append(jnp.stack(score_list))
    stacked = jnp.stack(all_grads)
    received = jnp.roll(stacked, -1, axis=0)
    return received, jnp.stack(all_scores)
```

```python
import jax
import jax.numpy as jnp
from jax import lax
from jax.experimental import pallas as pl
from jax.experimental.pallas import tpu as pltpu
from jax.sharding import PartitionSpec as P


def expert_kernel(x_ref, g_ref, gate_ref, wgu_ref, wdt_ref, wgut_ref, out_ref, score_ref):
    hidden = wdt_ref.shape[1]
    pre = jnp.dot(x_ref[...], wgu_ref[...], preferred_element_type=jnp.float32)
    gate_pre = pre[:, :hidden]
    up_pre = pre[:, hidden:]
    back = jnp.dot(g_ref[...], wdt_ref[...], preferred_element_type=jnp.float32)
    logistic = 1.0 / (1.0 + jnp.exp(-gate_pre))
    swish = gate_pre * logistic
    d_up = back * swish
    score_ref[...] = jnp.sum(d_up * up_pre, axis=1, keepdims=True)
    d_gate = back * up_pre * logistic * (1.0 + gate_pre * (1.0 - logistic))
    both = jnp.concatenate([d_gate.astype(jnp.bfloat16), d_up.astype(jnp.bfloat16)], axis=1)
    pair = jnp.dot(both, wgut_ref[...], preferred_element_type=jnp.float32)
    pair = pair.astype(jnp.bfloat16).astype(jnp.float32)
    out_ref[...] = (gate_ref[...] * pair).astype(jnp.bfloat16)


def expert_all(x, g, gate, wgu, wdt, wgut):
    rows, width = x.shape
    hidden = wdt.shape[1]
    block = min(512, rows)
    whole = lambda a: pl.BlockSpec(a.shape, lambda i: (0, 0), pipeline_mode=pl.Buffered(1))
    part = lambda cols: pl.BlockSpec((block, cols), lambda i: (i, 0))
    return pl.pallas_call(
        expert_kernel,
        grid=(rows // block,),
        in_specs=[part(width), part(width), part(1), whole(wgu), whole(wdt), whole(wgut)],
        out_specs=[part(width), part(1)],
        out_shape=[
            jax.ShapeDtypeStruct((rows, width), jnp.bfloat16),
            jax.ShapeDtypeStruct((rows, 1), jnp.float32),
        ],
        compiler_params=pltpu.CompilerParams(vmem_limit_bytes=56 * 1024 * 1024),
        cost_estimate=pl.CostEstimate(
            flops=10 * rows * width * hidden,
            bytes_accessed=rows * width * 6 + 10 * width * hidden,
            transcendentals=rows * hidden,
        ),
    )(x, g, gate, wgu, wdt, wgut)


def on_device(inputs, grads_out, expert_ids, gate_values, w_gate, w_up, w_down):
    experts = lax.axis_size("expert")
    x_all, grad_all = inputs[0], grads_out[0]
    ids_all, gates_all = expert_ids[0], gate_values[0]
    micro_count, rows, width = x_all.shape
    onehot = ids_all[:, :, :, None] == jnp.arange(experts, dtype=jnp.int32)
    dense = jnp.sum(jnp.where(onehot, gates_all[..., None], 0.0), axis=2)
    dense = jnp.transpose(dense, (2, 0, 1))
    dense = lax.all_to_all(dense, "expert", split_axis=0, concat_axis=0, tiled=True)
    wgu = jnp.concatenate([w_gate[0, 0], w_up[0, 0]], axis=1)
    wgut = wgu.T
    wdt = w_down[0, 0].T
    delivered, scores = [], []
    gathered = []
    for micro in range(micro_count):
        gathered.append(
            (
                lax.all_gather(x_all[micro], "expert", axis=0, tiled=True),
                lax.all_gather(grad_all[micro], "expert", axis=0, tiled=True),
            )
        )
    for micro in range(micro_count):
        x, g = gathered[micro]
        out, score = expert_all(x, g, dense[:, micro].reshape(-1, 1), wgu, wdt, wgut)
        total = lax.psum_scatter(out, "expert", scatter_dimension=0, tiled=True)
        delivered.append(
            (grad_all[micro].astype(jnp.float32) + total.astype(jnp.float32)).astype(jnp.bfloat16)
        )
        scores.append(score.reshape(experts, rows).astype(jnp.bfloat16))
    back = lax.all_to_all(
        jnp.stack(scores, axis=1), "expert", split_axis=0, concat_axis=0, tiled=True
    )
    back = jnp.transpose(back, (1, 2, 0)).astype(jnp.float32)
    gate_grad = jnp.sum(jnp.where(onehot, back[:, :, None, :], 0.0), axis=3)
    received = jnp.stack(delivered)[None]
    count = lax.axis_size("pipe")
    received = lax.ppermute(received, "pipe", [(s, (s - 1) % count) for s in range(count)])
    return (received, gate_grad[None])


def solution(mesh):
    tokens = P("pipe", None, "expert", None)
    weights = P("pipe", "expert", None, None)
    return jax.shard_map(
        on_device,
        mesh=mesh,
        in_specs=(tokens,) * 4 + (weights,) * 3,
        out_specs=(tokens, tokens),
        check_vma=False,
    )
```

```python
import functools

import jax
import jax.numpy as jnp
from jax import lax
from jax.experimental import pallas as pl
from jax.experimental.pallas import tpu as pltpu
from jax.sharding import PartitionSpec as P

LANES = 128
NT = (((1,), (1,)), ((), ()))


def across(value, step, bits):
    total, scale = 0, 1
    for _ in range(bits):
        total = total + scale * (((value // scale) % 2 + (step // scale) % 2) % 2)
        scale = 2 * scale
    return total


def section_kernel(
    layers, payload, wg_hbm, wu_hbm, wd_hbm,
    out_ref, score_ref, gathered,
    wg, wu, wd, xv, acc, staged, plane_in, layer_out, layer_in,
    w_loc, w_send, w_recv, loc, z_send, z_recv, a_send, a_recv, f_send, f_recv,
    r_send, r_recv, l_send, l_recv,
):
    bits = layers.bit_length() - 1
    me = lax.axis_index("expert")
    z, place = me // 8, me % 8
    y, x, core = place // 4, (place // 2) % 2, place % 2

    def at(layer, row, column, side):
        return ((layer * 2 + row) * 2 + column) * 2 + side

    partner = at(z, y, x, 1 - core)
    peers = [at(z, y, 1 - x, core), at(z, 1 - y, x, core), at(z, 1 - y, 1 - x, core)]

    def layer_peer(step):
        return at(across(z, step, bits), y, x, core)

    def remote(src, dst, send, recv, device):
        return pltpu.make_async_remote_copy(
            src_ref=src, dst_ref=dst, send_sem=send, recv_sem=recv,
            device_id={"expert": device}, device_id_type=pl.DeviceIdType.MESH,
        )

    rows = payload.shape[1]
    width = out_ref.shape[1]
    many = 4 * rows

    def weight_copy(i):
        return remote(
            (wg_hbm, wu_hbm, wd_hbm)[i], (wg, wu, wd)[i].at[1], w_send.at[i], w_recv.at[i], partner
        )

    def weight_local(i):
        return pltpu.make_async_copy(
            (wg_hbm, wu_hbm, wd_hbm)[i], (wg, wu, wd)[i].at[0], w_loc.at[i]
        )

    def layer_gather(step):
        return remote(
            payload, gathered.at[step, 0], z_send.at[step], z_recv.at[step], layer_peer(step)
        )

    def plane_gather(step, side):
        return remote(
            gathered.at[step, 0], gathered.at[step, 1 + side],
            a_send.at[step, side], a_recv.at[step, side], peers[side],
        )

    def forward(step, side):
        return remote(
            gathered.at[step, 1 + side, side], gathered.at[step, 3, side],
            f_send.at[step, side], f_recv.at[step, side], peers[1 - side],
        )

    def plane_reduce(step, k):
        return remote(
            staged.at[step % 2, 1 + k], plane_in.at[step, k],
            r_send.at[step, k], r_recv.at[step, k], peers[k],
        )

    def layer_reduce(step):
        return remote(
            layer_out.at[step], layer_in.at[step], l_send.at[step], l_recv.at[step],
            layer_peer(step),
        )

    barrier = pltpu.get_barrier_semaphore()
    greeted = [partner] + peers + [layer_peer(s) for s in range(1, layers)]
    for device in greeted:
        pl.semaphore_signal(
            barrier, inc=1, device_id={"expert": device}, device_id_type=pl.DeviceIdType.MESH
        )
    first = pltpu.make_async_copy(payload, gathered.at[0, 0], loc.at[0])
    first.start()
    first.wait()
    for i in range(3):
        weight_local(i).start()
    pl.semaphore_wait(barrier, len(greeted))

    for side in range(2):
        plane_gather(0, side).start()
    if layers > 1:
        layer_gather(1).start()
    for i in range(3):
        weight_copy(i).start()
    for side in range(2):
        plane_gather(0, side).wait_recv()
        forward(0, side).start()

    lane = lax.broadcasted_iota(jnp.int32, (many, LANES), 1)

    def expert(j, expert_id, slot):
        xs = xv[:, 0, :, :width].reshape(many, width)
        gs = xv[:, 1, :, :width].reshape(many, width)
        gate_pre = jnp.dot(xs, wg[j], preferred_element_type=jnp.float32)
        up_pre = jnp.dot(xs, wu[j], preferred_element_type=jnp.float32)
        back = lax.dot_general(gs, wd[j], NT, preferred_element_type=jnp.float32)
        logistic = 1.0 / (1.0 + jnp.exp(-gate_pre))
        swish = gate_pre * logistic
        d_up = back * swish
        score = jnp.sum(d_up * up_pre, axis=1, keepdims=True)
        d_gate = (back * up_pre * logistic * (1.0 + gate_pre * (1.0 - logistic)))
        d_gate, d_up = d_gate.astype(jnp.bfloat16), d_up.astype(jnp.bfloat16)
        gates = xv[:, :, :, width:].astype(jnp.float32)
        gates = (gates[:, 0] + gates[:, 1]).reshape(many, LANES)
        gate = jnp.sum(jnp.where(lane == expert_id, gates, 0.0), axis=1, keepdims=True)
        spread = jnp.where(lane == expert_id, score, 0.0)
        tile = min(512, width)
        for col in range(0, width, tile):
            cols = pl.ds(col, tile)
            pair = lax.dot_general(d_gate, wg[j, cols, :], NT, preferred_element_type=jnp.float32)
            pair = pair + lax.dot_general(
                d_up, wu[j, cols, :], NT, preferred_element_type=jnp.float32
            )
            pair = gate * pair.astype(jnp.bfloat16).astype(jnp.float32)
            if j == 0:
                acc[:, cols] = pair
            else:
                staged[slot, :, :, cols] = (
                    (acc[:, cols] + pair).astype(jnp.bfloat16).reshape(4, rows, tile)
                )
        cols = pl.ds(width, LANES)
        if j == 0:
            acc[:, cols] = spread
        else:
            staged[slot, :, :, cols] = (
                (acc[:, cols] + spread).astype(jnp.bfloat16).reshape(4, rows, LANES)
            )

    def finish_plane(step):
        for k in range(3):
            plane_reduce(step, k).wait_send()
            plane_reduce(step, k).wait_recv()
        total = staged[step % 2, 0].astype(jnp.float32)
        for k in range(3):
            total = total + plane_in[step, k].astype(jnp.float32)
        layer_out[step] = total.astype(jnp.bfloat16)

        @pl.when(step > 0)
        def _():
            layer_reduce(step).start()

    def one_step(step, carry):
        @pl.when(step + 1 < layers)
        def _():
            layer_gather(step + 1).wait_recv()
            for side in range(2):
                plane_gather(step + 1, side).start()

        @pl.when(step + 2 < layers)
        def _():
            layer_gather(step + 2).start()

        for side in range(2):
            forward(step, side).wait_recv()
        load = pltpu.make_async_copy(gathered.at[step], xv, loc.at[1])
        load.start()
        load.wait()

        @pl.when(step == 0)
        def _():
            for i in range(3):
                weight_local(i).wait()

        expert(0, me, step % 2)

        @pl.when(step + 1 < layers)
        def _():
            for side in range(2):
                plane_gather(step + 1, side).wait_recv()
                forward(step + 1, side).start()

        @pl.when(step == 0)
        def _():
            for i in range(3):
                weight_copy(i).wait_recv()

        expert(1, partner, step % 2)
        for k in range(3):
            plane_reduce(step, k).start()

        @pl.when(step > 0)
        def _():
            finish_plane(step - 1)

        return carry

    lax.fori_loop(0, layers, one_step, 0)
    finish_plane(layers - 1)

    total = layer_out[0].astype(jnp.float32)
    for step in range(1, layers):
        layer_reduce(step).wait_recv()
        total = total + layer_in[step].astype(jnp.float32)
    own = xv.at[0, 1]
    grads = pltpu.make_async_copy(payload.at[1], own, loc.at[0])
    grads.start()
    grads.wait()
    out_ref[...] = (own[:, :width].astype(jnp.float32) + total[:, :width]).astype(jnp.bfloat16)
    score_ref[...] = total[:, width:].astype(jnp.bfloat16)

    for i in range(3):
        weight_copy(i).wait_send()
    for step in range(layers):
        for side in range(2):
            plane_gather(step, side).wait_send()
            forward(step, side).wait_send()
        if step > 0:
            layer_gather(step).wait_send()
            layer_reduce(step).wait_send()


def section(payload, w_gate, w_up, w_down, experts):
    layers = experts // 8
    _, rows, wide = payload.shape
    width, hidden = w_gate.shape
    bf16 = jnp.bfloat16
    sem = pltpu.SemaphoreType.DMA
    anywhere = pl.BlockSpec(memory_space=pl.ANY)
    vmem = pl.BlockSpec(memory_space=pltpu.VMEM)
    out, score, _ = pl.pallas_call(
        functools.partial(section_kernel, layers),
        in_specs=[anywhere] * 4,
        out_specs=[vmem, vmem, anywhere],
        out_shape=[
            jax.ShapeDtypeStruct((rows, width), bf16),
            jax.ShapeDtypeStruct((rows, LANES), bf16),
            jax.ShapeDtypeStruct((layers, 4, 2, rows, wide), bf16),
        ],
        scratch_shapes=[
            pltpu.VMEM((2, width, hidden), bf16),
            pltpu.VMEM((2, width, hidden), bf16),
            pltpu.VMEM((2, hidden, width), bf16),
            pltpu.VMEM((4, 2, rows, wide), bf16),
            pltpu.VMEM((4 * rows, wide), jnp.float32),
            pltpu.VMEM((2, 4, rows, wide), bf16),
            pltpu.VMEM((layers, 3, rows, wide), bf16),
            pltpu.VMEM((layers, rows, wide), bf16),
            pltpu.VMEM((layers, rows, wide), bf16),
            sem((3,)), sem((3,)), sem((3,)), sem((2,)),
            sem((layers,)), sem((layers,)),
            sem((layers, 2)), sem((layers, 2)),
            sem((layers, 2)), sem((layers, 2)),
            sem((layers, 3)), sem((layers, 3)),
            sem((layers,)), sem((layers,)),
        ],
        compiler_params=pltpu.CompilerParams(
            collective_id=0, has_side_effects=True, vmem_limit_bytes=63 * 1024 * 1024
        ),
    )(payload, w_gate, w_up, w_down)
    return out, score


def on_device(inputs, grads_out, expert_ids, gate_values, w_gate, w_up, w_down):
    experts = lax.axis_size("expert")
    x_all, grad_all = inputs[0], grads_out[0]
    micro, rows, width = x_all.shape
    count = micro * rows
    picks = expert_ids.shape[3]
    ids = expert_ids.reshape(count, picks)
    gates = gate_values.reshape(count, picks)
    onehot = ids[:, :, None] == jnp.arange(LANES, dtype=jnp.int32)
    dense = jnp.sum(jnp.where(onehot, gates[..., None], 0.0), axis=1)
    high = lax.reduce_precision(dense, 8, 7)
    low = (dense - high).astype(jnp.bfloat16)
    payload = jnp.stack(
        [
            jnp.concatenate([x_all.reshape(count, width), high.astype(jnp.bfloat16)], axis=1),
            jnp.concatenate([grad_all.reshape(count, width), low], axis=1),
        ]
    )
    out, score = section(payload, w_gate[0, 0], w_up[0, 0], w_down[0, 0], experts)
    gate_grad = jnp.sum(jnp.where(onehot, score.astype(jnp.float32)[:, None, :], 0.0), axis=2)
    received = out.reshape(1, micro, rows, width)
    sections = lax.axis_size("pipe")
    if sections > 1:
        received = lax.ppermute(
            received, "pipe", [(s, (s - 1) % sections) for s in range(sections)]
        )
    return (received, gate_grad.reshape(1, micro, rows, picks))


def solution(mesh):
    tokens = P("pipe", None, "expert", None)
    weights = P("pipe", "expert", None, None)
    return jax.shard_map(
        on_device,
        mesh=mesh,
        in_specs=(tokens,) * 4 + (weights,) * 3,
        out_specs=(tokens, tokens),
        check_vma=False,
    )
```

```python
import functools

import jax
import jax.numpy as jnp
from jax import lax
from jax.experimental import pallas as pl
from jax.experimental.pallas import tpu as pltpu
from jax.sharding import PartitionSpec as P

LANES = 128
NT = (((1,), (1,)), ((), ()))


def across(value, step, bits):
    total, scale = 0, 1
    for _ in range(bits):
        total = total + scale * (((value // scale) % 2 + (step // scale) % 2) % 2)
        scale = 2 * scale
    return total


def section_kernel(
    layers, payload, wg_hbm, wu_hbm, wd_hbm,
    out_ref, score_ref, gathered,
    wg, wu, wd, xv, acc, staged, plane_in, diag_in, layer_out, layer_in,
    w_loc, w_send, w_recv, loc, z_send, z_recv, a_send, a_recv, f_send, f_recv,
    r_send, r_recv, l_send, l_recv,
):
    bits = layers.bit_length() - 1
    me = lax.axis_index("expert")
    z, place = me // 8, me % 8
    y, x, core = place // 4, (place // 2) % 2, place % 2

    def at(layer, row, column, side):
        return ((layer * 2 + row) * 2 + column) * 2 + side

    partner = at(z, y, x, 1 - core)
    peers = [at(z, y, 1 - x, core), at(z, 1 - y, x, core), at(z, 1 - y, 1 - x, core)]

    def layer_peer(step):
        return at(across(z, step, bits), y, x, core)

    def remote(src, dst, send, recv, device):
        return pltpu.make_async_remote_copy(
            src_ref=src, dst_ref=dst, send_sem=send, recv_sem=recv,
            device_id={"expert": device}, device_id_type=pl.DeviceIdType.MESH,
        )

    rows = payload.shape[1]
    width = out_ref.shape[1]
    many = 4 * rows
    half = rows // 2

    def weight_copy(i):
        return remote(
            (wg_hbm, wu_hbm, wd_hbm)[i], (wg, wu, wd)[i].at[1], w_send.at[i], w_recv.at[i], partner
        )

    def weight_local(i):
        return pltpu.make_async_copy(
            (wg_hbm, wu_hbm, wd_hbm)[i], (wg, wu, wd)[i].at[0], w_loc.at[i]
        )

    def layer_gather(step):
        return remote(
            payload, gathered.at[step, 0], z_send.at[step], z_recv.at[step], layer_peer(step)
        )

    def plane_gather(step, side):
        return remote(
            gathered.at[step, 0], gathered.at[step, 1 + side],
            a_send.at[step, side], a_recv.at[step, side], peers[side],
        )

    def forward(step, side):
        return remote(
            gathered.at[step, 1 + side, side], gathered.at[step, 3, side],
            f_send.at[step, side], f_recv.at[step, side], peers[1 - side],
        )

    def plane_reduce(step, k):
        return remote(
            staged.at[step % 2, 1 + k], plane_in.at[step, k],
            r_send.at[step, k], r_recv.at[step, k], peers[k],
        )

    def diag_reduce(step, side):
        return remote(
            staged.at[step % 2, 3, pl.ds(side * half, half)], diag_in.at[step, side],
            r_send.at[step, 2 + side], r_recv.at[step, 2 + side], peers[side],
        )

    def layer_reduce(step):
        return remote(
            layer_out.at[step], layer_in.at[step], l_send.at[step], l_recv.at[step],
            layer_peer(step),
        )

    barrier = pltpu.get_barrier_semaphore()
    greeted = [partner] + peers + [layer_peer(s) for s in range(1, layers)]
    for device in greeted:
        pl.semaphore_signal(
            barrier, inc=1, device_id={"expert": device}, device_id_type=pl.DeviceIdType.MESH
        )
    first = pltpu.make_async_copy(payload, gathered.at[0, 0], loc.at[0])
    first.start()
    first.wait()
    for i in range(3):
        weight_local(i).start()
    pl.semaphore_wait(barrier, len(greeted))

    for side in range(2):
        plane_gather(0, side).start()
    if layers > 1:
        layer_gather(1).start()
    for i in range(3):
        weight_copy(i).start()
    for side in range(2):
        plane_gather(0, side).wait_recv()
        forward(0, side).start()

    lane = lax.broadcasted_iota(jnp.int32, (many, LANES), 1)

    def expert(j, expert_id, slot):
        xs = xv[:, 0, :, :width].reshape(many, width)
        gs = xv[:, 1, :, :width].reshape(many, width)
        gate_pre = jnp.dot(xs, wg[j], preferred_element_type=jnp.float32)
        up_pre = jnp.dot(xs, wu[j], preferred_element_type=jnp.float32)
        back = lax.dot_general(gs, wd[j], NT, preferred_element_type=jnp.float32)
        logistic = 1.0 / (1.0 + jnp.exp(-gate_pre))
        swish = gate_pre * logistic
        d_up = back * swish
        score = jnp.sum(d_up * up_pre, axis=1, keepdims=True)
        d_gate = (back * up_pre * logistic * (1.0 + gate_pre * (1.0 - logistic)))
        d_gate, d_up = d_gate.astype(jnp.bfloat16), d_up.astype(jnp.bfloat16)
        gates = xv[:, :, :, width:].astype(jnp.float32)
        gates = (gates[:, 0] + gates[:, 1]).reshape(many, LANES)
        gate = jnp.sum(jnp.where(lane == expert_id, gates, 0.0), axis=1, keepdims=True)
        spread = jnp.where(lane == expert_id, score, 0.0)
        tile = min(512, width)
        for col in range(0, width, tile):
            cols = pl.ds(col, tile)
            pair = lax.dot_general(d_gate, wg[j, cols, :], NT, preferred_element_type=jnp.float32)
            pair = pair + lax.dot_general(
                d_up, wu[j, cols, :], NT, preferred_element_type=jnp.float32
            )
            pair = gate * pair.astype(jnp.bfloat16).astype(jnp.float32)
            if j == 0:
                acc[:, cols] = pair
            else:
                staged[slot, :, :, cols] = (
                    (acc[:, cols] + pair).astype(jnp.bfloat16).reshape(4, rows, tile)
                )
        cols = pl.ds(width, LANES)
        if j == 0:
            acc[:, cols] = spread
        else:
            staged[slot, :, :, cols] = (
                (acc[:, cols] + spread).astype(jnp.bfloat16).reshape(4, rows, LANES)
            )

    def merge_plane(step):
        for side in range(2):
            diag_reduce(step, side).wait_send()
            diag_reduce(step, side).wait_recv()
            part = pl.ds(side * half, half)
            merged = staged[step % 2, 2 - side, part].astype(jnp.float32)
            merged = merged + diag_in[step, side].astype(jnp.float32)
            staged[step % 2, 2 - side, part] = merged.astype(jnp.bfloat16)
        for k in range(2):
            plane_reduce(step, k).start()

    def finish_plane(step):
        for k in range(2):
            plane_reduce(step, k).wait_send()
            plane_reduce(step, k).wait_recv()
        total = staged[step % 2, 0].astype(jnp.float32)
        for k in range(2):
            total = total + plane_in[step, k].astype(jnp.float32)
        layer_out[step] = total.astype(jnp.bfloat16)

        @pl.when(step > 0)
        def _():
            layer_reduce(step).start()

    def one_step(step, carry):
        @pl.when(step + 1 < layers)
        def _():
            layer_gather(step + 1).wait_recv()
            for side in range(2):
                plane_gather(step + 1, side).start()

        @pl.when(step + 2 < layers)
        def _():
            layer_gather(step + 2).start()

        for side in range(2):
            forward(step, side).wait_recv()
        load = pltpu.make_async_copy(gathered.at[step], xv, loc.at[1])
        load.start()
        load.wait()

        @pl.when(step == 0)
        def _():
            for i in range(3):
                weight_local(i).wait()

        expert(0, me, step % 2)

        @pl.when(step + 1 < layers)
        def _():
            for side in range(2):
                plane_gather(step + 1, side).wait_recv()
                forward(step + 1, side).start()

        @pl.when(step == 0)
        def _():
            for i in range(3):
                weight_copy(i).wait_recv()

        @pl.when(step > 1)
        def _():
            finish_plane(step - 2)

        @pl.when(step > 0)
        def _():
            merge_plane(step - 1)

        expert(1, partner, step % 2)
        for side in range(2):
            diag_reduce(step, side).start()

        return carry

    lax.fori_loop(0, layers, one_step, 0)
    if layers > 1:
        finish_plane(layers - 2)
    merge_plane(layers - 1)
    finish_plane(layers - 1)

    total = layer_out[0].astype(jnp.float32)
    for step in range(1, layers):
        layer_reduce(step).wait_recv()
        total = total + layer_in[step].astype(jnp.float32)
    own = xv.at[0, 1]
    grads = pltpu.make_async_copy(payload.at[1], own, loc.at[0])
    grads.start()
    grads.wait()
    out_ref[...] = (own[:, :width].astype(jnp.float32) + total[:, :width]).astype(jnp.bfloat16)
    score_ref[...] = total[:, width:].astype(jnp.bfloat16)

    for i in range(3):
        weight_copy(i).wait_send()
    for step in range(layers):
        for side in range(2):
            plane_gather(step, side).wait_send()
            forward(step, side).wait_send()
        if step > 0:
            layer_gather(step).wait_send()
            layer_reduce(step).wait_send()


def section(payload, w_gate, w_up, w_down, experts):
    layers = experts // 8
    _, rows, wide = payload.shape
    width, hidden = w_gate.shape
    bf16 = jnp.bfloat16
    sem = pltpu.SemaphoreType.DMA
    anywhere = pl.BlockSpec(memory_space=pl.ANY)
    vmem = pl.BlockSpec(memory_space=pltpu.VMEM)
    out, score, _ = pl.pallas_call(
        functools.partial(section_kernel, layers),
        in_specs=[anywhere] * 4,
        out_specs=[vmem, vmem, anywhere],
        out_shape=[
            jax.ShapeDtypeStruct((rows, width), bf16),
            jax.ShapeDtypeStruct((rows, LANES), bf16),
            jax.ShapeDtypeStruct((layers, 4, 2, rows, wide), bf16),
        ],
        scratch_shapes=[
            pltpu.VMEM((2, width, hidden), bf16),
            pltpu.VMEM((2, width, hidden), bf16),
            pltpu.VMEM((2, hidden, width), bf16),
            pltpu.VMEM((4, 2, rows, wide), bf16),
            pltpu.VMEM((4 * rows, wide), jnp.float32),
            pltpu.VMEM((2, 4, rows, wide), bf16),
            pltpu.VMEM((layers, 2, rows, wide), bf16),
            pltpu.VMEM((layers, 2, rows // 2, wide), bf16),
            pltpu.VMEM((layers, rows, wide), bf16),
            pltpu.VMEM((layers, rows, wide), bf16),
            sem((3,)), sem((3,)), sem((3,)), sem((2,)),
            sem((layers,)), sem((layers,)),
            sem((layers, 2)), sem((layers, 2)),
            sem((layers, 2)), sem((layers, 2)),
            sem((layers, 4)), sem((layers, 4)),
            sem((layers,)), sem((layers,)),
        ],
        compiler_params=pltpu.CompilerParams(
            collective_id=0, has_side_effects=True, vmem_limit_bytes=63 * 1024 * 1024
        ),
    )(payload, w_gate, w_up, w_down)
    return out, score


def on_device(inputs, grads_out, expert_ids, gate_values, w_gate, w_up, w_down):
    experts = lax.axis_size("expert")
    x_all, grad_all = inputs[0], grads_out[0]
    micro, rows, width = x_all.shape
    count = micro * rows
    picks = expert_ids.shape[3]
    ids = expert_ids.reshape(count, picks)
    gates = gate_values.reshape(count, picks)
    onehot = ids[:, :, None] == jnp.arange(LANES, dtype=jnp.int32)
    dense = jnp.sum(jnp.where(onehot, gates[..., None], 0.0), axis=1)
    high = lax.reduce_precision(dense, 8, 7)
    low = (dense - high).astype(jnp.bfloat16)
    payload = jnp.stack(
        [
            jnp.concatenate([x_all.reshape(count, width), high.astype(jnp.bfloat16)], axis=1),
            jnp.concatenate([grad_all.reshape(count, width), low], axis=1),
        ]
    )
    out, score = section(payload, w_gate[0, 0], w_up[0, 0], w_down[0, 0], experts)
    gate_grad = jnp.sum(jnp.where(onehot, score.astype(jnp.float32)[:, None, :], 0.0), axis=2)
    received = out.reshape(1, micro, rows, width)
    sections = lax.axis_size("pipe")
    if sections > 1:
        received = lax.ppermute(
            received, "pipe", [(s, (s - 1) % sections) for s in range(sections)]
        )
    return (received, gate_grad.reshape(1, micro, rows, picks))


def solution(mesh):
    tokens = P("pipe", None, "expert", None)
    weights = P("pipe", "expert", None, None)
    return jax.shard_map(
        on_device,
        mesh=mesh,
        in_specs=(tokens,) * 4 + (weights,) * 3,
        out_specs=(tokens, tokens),
        check_vma=False,
    )
```
